32 devices in a mesh: frame: 4 (over y, x), vox: 8 (over z, core).
Axes of the slice: x: 2, y: 2, z: 4, core: 2. Of those that a mesh axis runs over, the one named last changes fastest.
Arguments:
- pool: bfloat16 [2048, 8192], P('frame', 'vox'), may hold values from -6 to 6
- dictionary: bfloat16 [1024, 8192], P(None, 'vox'), may hold values from -0.13258252 to 0.13258252
- support: int32 [1024, 64], P(None, 'vox'), may hold values from 0 to 1, as said below
- pick: int32 [1024], P('frame'), may hold values from 0 to 511
Outputs:
- codes: bfloat16 [1024, 1024], P('frame')
- gradient: float32 [1024, 8192], P('frame', 'vox')
The draws below stay inside these ranges and needn't reach their ends.
Inputs may be any that keep to these rules, and one draw needn't show every extreme that they name: Every mode has at least one voxel block in its support.
All inputs are finite; a program needn't handle non-finite values.
Results may differ from the reference program's by a relative error of at most 0.015.
Values may be sent and summed in bfloat16 or wider, within the bound.
No kernel may reach another device: no remote copies, remote signals or barrier semaphores. Data moves between devices by JAX's collectives and lax.ppermute only.
A program may use at most 64 MiB of HBM per device.

```python
import jax
import jax.numpy as jnp
from jax import lax

MODES = 1024
BLOCK = 128
FRAME_DEV = 256
BLOCKS = 64
VOXELS = 8192
FRAMES = 1024
POOL = 2048
N_FRAME = 4


def draw_support(key, part):
    values = jax.random.randint(key, (MODES, BLOCKS), 0, 4)
    forced = jnp.arange(BLOCKS)[None, :] == jnp.arange(MODES)[:, None] % BLOCKS
    return jnp.where((values != 0) | forced, 1, 0).astype(jnp.int32)


def draw_dictionary(key, part):
    key_base = jax.random.fold_in(key, 11)
    key_mode = jax.random.fold_in(key, 12)
    key_block = jax.random.fold_in(key, 13)
    base = jnp.clip(jax.random.normal(key_base, (MODES, VOXELS), jnp.float32), -4.0, 4.0)
    mode_lo, mode_hi = (0.55, 1.8)
    mode_level = jnp.exp(jax.random.uniform(key_mode, (MODES, 1), jnp.float32, jnp.log(mode_lo), jnp.log(mode_hi)))
    block_level = jnp.exp(jax.random.uniform(key_block, (MODES, BLOCKS), jnp.float32, jnp.log(0.6), jnp.log(1.6)))
    block_wide = jnp.repeat(block_level, BLOCK, axis=1)
    scale = 1.0 / jnp.sqrt(jnp.float32(VOXELS))
    return (base * mode_level * block_wide * scale).astype(jnp.bfloat16)


def touch_ends(entries, rng, low, largest):
    dims = entries.shape
    spot = [jax.random.randint(jax.random.fold_in(rng, axis), (), 0, dims[axis]) for axis in range(len(dims))]
    entries = entries.at[tuple(spot)].set(low)
    longest = dims.index(max(dims))
    spot[longest] = (spot[longest] + 1) % dims[longest]
    return entries.at[tuple(spot)].set(largest)


def level_of(stream_key, dims, pieces, least, largest):
    def one(axis_at, parts):
        steps = jax.random.uniform(jax.random.fold_in(jax.random.fold_in(stream_key, 6), axis_at), (parts,), jnp.float32, least / len(pieces), largest / len(pieces))
        return jnp.repeat(jnp.exp(steps), dims[axis_at] // parts).reshape((-1,) + (1,) * (len(dims) - axis_at - 1))

    factor_of = one(*pieces[0])
    for cut in pieces[1:]:
        factor_of = factor_of * one(*cut)
    return factor_of


def scatter_about(stream_key, dims, width, most, shards=(), kind=jnp.bfloat16):
    result = width * jax.random.normal(stream_key, dims, jnp.float32)
    if shards:
        result = result * level_of(stream_key, dims, shards, -0.22, 0.18)
    return jnp.clip(result, -most, most).astype(kind)


def setup_inputs(seed: int = 0) -> dict:
    seeds = jax.random.split(jax.random.key(seed), 5)
    pool = scatter_about(seeds[0], (POOL, VOXELS), 1.0, 6.0, ((0, 4), (1, 8)))
    dictionary = draw_dictionary(jax.random.fold_in(seeds[4], 71), 0)
    support = draw_support(jax.random.fold_in(seeds[4], 71), 0)
    pick = touch_ends(jax.random.randint(seeds[3], (FRAMES,), 0, 2 * FRAME_DEV), jax.random.fold_in(seeds[3], 1), 0, (2 * FRAME_DEV) - 1).astype(jnp.int32)
    return dict(pool=pool, dictionary=dictionary, support=support, pick=pick)


def shrink(value, limit):
    return jnp.sign(value) * jnp.maximum(jnp.abs(value) - limit, 0.0)


def reference(pool, dictionary, support, pick):
    rows = (jnp.arange(FRAMES, dtype=jnp.int32) // FRAME_DEV) * (2 * FRAME_DEV) + pick
    batch = pool[rows]
    keep = jnp.repeat(support, BLOCK, axis=1).astype(jnp.bfloat16)
    masked = dictionary * keep
    corr = jnp.dot(batch, masked.T, preferred_element_type=jnp.float32)
    energy = jnp.sum(jnp.square(masked.astype(jnp.float32)), axis=1)
    step = 1.0 / (energy + 1e-5)
    first = shrink(corr * step, 0.3 * step).astype(jnp.bfloat16)
    resid = (jnp.dot(first, masked, preferred_element_type=jnp.float32) - batch.astype(jnp.float32)).astype(jnp.bfloat16)
    push = jnp.dot(resid, masked.T, preferred_element_type=jnp.float32)
    codes = shrink(first.astype(jnp.float32) - step * push, 0.3 * step).astype(jnp.bfloat16)
    error = (jnp.dot(codes, masked, preferred_element_type=jnp.float32) - batch.astype(jnp.float32)).astype(jnp.bfloat16)
    code_groups = codes.reshape(N_FRAME, FRAME_DEV, MODES)
    error_groups = error.reshape(N_FRAME, FRAME_DEV, VOXELS)

    def add_group(total, pair):
        part = jnp.dot(pair[0].T, pair[1], preferred_element_type=jnp.float32).astype(jnp.bfloat16)
        return total + part.astype(jnp.float32), None

    total, _ = lax.scan(add_group, jnp.zeros((MODES, VOXELS), jnp.float32), (code_groups, error_groups))
    gradient = keep.astype(jnp.float32) * total / FRAMES
    return codes, gradient
```

```python
import functools

import jax
import jax.numpy as jnp
from jax import lax
from jax.experimental import pallas as pl
from jax.experimental.pallas import tpu as pltpu
from jax.sharding import PartitionSpec as P

LANE = 128
EXTRA = 16
BF = jnp.bfloat16
F32 = jnp.float32


def mm(left, right, a, b):
    return lax.dot_general(left, right, (((a,), (b,)), ((), ())), preferred_element_type=F32)


def shrink(value, limit):
    return value - jnp.clip(value, -limit, limit)


def expand_keep(sup, width):
    blocks = sup.shape[0]
    row = lax.broadcasted_iota(jnp.int32, (blocks, width), 0)
    col = lax.broadcasted_iota(jnp.int32, (blocks, width), 1)
    spread = jnp.where(col // (width // blocks) == row, 1.0, 0.0).astype(BF)
    return mm(sup.astype(F32).astype(BF), spread, 0, 0).astype(BF)


def split_rows(total):
    hi = total.astype(BF)
    rest = total - hi.astype(F32)
    mid = rest.astype(BF)
    low = (rest - mid.astype(F32)).astype(BF)
    row = lax.broadcasted_iota(jnp.int32, (EXTRA, LANE), 0)
    out = jnp.where(row == 0, hi.astype(F32), 0.0)
    out = jnp.where(row == 1, mid.astype(F32), out)
    return jnp.where(row == 2, low.astype(F32), out)


def block_of(index, size):
    return pl.ds(pl.multiple_of(index * size, size), size)


def prepare(pool, dic, sup, pick, batch, masked, keep, send, lhs):
    v, f = lax.axis_index("vox"), lax.axis_index("frame")
    frames, width = batch.shape
    modes = dic.shape[0]
    own = lhs.shape[0] - frames
    source = lax.broadcasted_iota(jnp.int32, (pool.shape[0], frames), 0)
    chosen = jnp.where(source == pick[...], 1.0, 0.0).astype(BF)
    rows = mm(chosen, pool[...], 0, 0).astype(BF)
    batch[...] = rows
    lhs[:frames, :] = rows
    for m in range(modes // LANE):
        at = slice(m * LANE, (m + 1) * LANE)
        masked[at, :] = dic[at, :] * expand_keep(sup[:, at], width)
    lhs[frames:, :] = masked[block_of(f, own), :]
    ones = jnp.ones((8, width), BF)
    for r in range(modes // LANE):
        block = masked[block_of((v % (modes // LANE)) ^ r, LANE), :]
        part = mm(lhs[...], block, 1, 1)
        square = jnp.square(block.astype(F32))
        hi = square.astype(BF)
        lo = (square - hi.astype(F32)).astype(BF)
        energy = (mm(ones, hi, 1, 1) + mm(ones, lo, 1, 1))[:1]
        height = part.shape[0]
        if r % 2:
            send[r // 2, :height, :] = part.astype(BF)
            send[r // 2, height:, :] = split_rows(energy).astype(BF)
        else:
            row = lax.broadcasted_iota(jnp.int32, (EXTRA, LANE), 0)
            keep[r // 2, :height, :] = part
            keep[r // 2, height:, :] = jnp.where(row == 0, energy, 0.0)


def fold_core(keep, got, own, *sends):
    height = own.shape[0] - EXTRA
    own[...] = keep[0] + got[0].astype(F32)
    for i, out in enumerate(sends):
        total = keep[i + 1] + got[i + 1].astype(F32)
        out[:height, :] = total[:height].astype(BF)
        out[height:, :] = split_rows(jnp.sum(total[height:], axis=0, keepdims=True)).astype(BF)


def fold_line(own, *rest):
    *gots, first, corr, step, gram = rest
    frames = first.shape[0]
    total = own[...]
    for got in gots:
        total = total + got[...].astype(F32)
    energy = jnp.sum(total[total.shape[0] - EXTRA :], axis=0, keepdims=True)
    scale = 1.0 / (energy + 1e-05)
    corr[...] = total[:frames]
    first[...] = shrink(total[:frames] * scale, 0.3 * scale).astype(BF)
    step[...] = jnp.broadcast_to(scale, step.shape)
    gram[...] = total[frames : total.shape[0] - EXTRA].astype(BF)


def second(n_first, n_gram, *refs):
    firsts = refs[:n_first]
    grams = refs[n_first : n_first + n_gram]
    corr, step, codes, square = refs[n_first + n_gram :]
    v, f = lax.axis_index("vox"), lax.axis_index("frame")
    own = grams[0].shape[0]
    for s in range(n_gram):
        square[block_of(f ^ s, own), :] = grams[s][...]
    push = -corr[...]
    for r in range(n_first):
        push = push + mm(firsts[r][...], square[block_of((v % n_first) ^ r, LANE), :], 1, 0)
    scale = step[:1, :]
    codes[...] = shrink(firsts[0][...].astype(F32) - scale * push, 0.3 * scale).astype(BF)


def pack(*refs):
    *parts, out = refs
    for i, part in enumerate(parts):
        out[i] = part[...]


def place(half, other, whole):
    v = lax.axis_index("vox")
    count = half.shape[0]
    for i in range(count):
        whole[:, block_of((v % (2 * count)) ^ (2 * i), LANE)] = half[i]
        whole[:, block_of((v % (2 * count)) ^ (2 * i + 1), LANE)] = other[i]


def own_group(half, other, masked, batch, codes, total):
    f = lax.axis_index("frame")
    place(half, other, codes)
    error = (mm(codes[...], masked[...], 1, 0) - batch[...].astype(F32)).astype(BF)
    rows = total.shape[0]
    total[...] = mm(codes[:, block_of(f, rows)], error, 0, 0)


def last_groups(n, scale, *refs):
    halves, others, batches = refs[:n], refs[n : 2 * n], refs[2 * n : 3 * n]
    masked, sup, total, gradient, codes = refs[3 * n :]
    f = lax.axis_index("frame")
    rows = total.shape[0]
    acc = total[...]
    for i in range(n):
        place(halves[i], others[i], codes)
        error = (mm(codes[...], masked[...], 1, 0) - batches[i][...].astype(F32)).astype(BF)
        acc = acc + mm(codes[:, block_of(f, rows)], error, 0, 0)
    kept = expand_keep(sup[:, block_of(f, rows)], total.shape[1]).astype(F32)
    gradient[...] = kept * acc * scale


def call(kernel, outs, args, scratch=(), flops=0):
    moved = sum(a.size * a.dtype.itemsize for a in (*args, *outs))
    single = len(outs) == 1
    return pl.pallas_call(
        kernel,
        out_shape=outs[0] if single else outs,
        in_specs=[pl.BlockSpec(memory_space=pltpu.VMEM)] * len(args),
        out_specs=pl.BlockSpec(memory_space=pltpu.VMEM)
        if single
        else [pl.BlockSpec(memory_space=pltpu.VMEM)] * len(outs),
        scratch_shapes=list(scratch),
        cost_estimate=pl.CostEstimate(flops=flops, bytes_accessed=moved, transcendentals=0),
    )(*args)


def shape(dims, dtype):
    return jax.ShapeDtypeStruct(dims, dtype)


def body(pool, dictionary, support, pick):
    n_vox, n_frame = lax.axis_size("vox"), lax.axis_size("frame")
    modes, width = dictionary.shape
    frames = pick.shape[0]
    blocks = modes // LANE
    own = modes // n_frame
    height = frames + own + EXTRA
    line = [m for m in range(2, blocks, 2)]

    def hop(x, axis, m):
        n = n_vox if axis == "vox" else n_frame
        return lax.ppermute(x, axis, [(k, k ^ m) for k in range(n)])

    sup = support.T
    batch, masked, keep, send = call(
        prepare,
        [
            shape((frames, width), BF),
            shape((modes, width), BF),
            shape((blocks // 2, height, LANE), F32),
            shape((blocks // 2, height, LANE), BF),
        ],
        (pool, dictionary, sup, pick.reshape(1, frames)),
        [pltpu.VMEM((frames + own, width), BF)],
        2 * (frames + own) * modes * width,
    )
    got = hop(send, "vox", 1)
    mine, *sends = call(
        fold_core,
        [shape((height, LANE), F32)] + [shape((height, LANE), BF)] * len(line),
        (keep, got),
    )
    gots = [hop(s, "vox", m) for s, m in zip(sends, line)]
    far = blocks
    while far < n_vox:
        total = mine
        for g in gots:
            total = total + g.astype(F32)
        top, end = total[:-EXTRA].astype(BF), jnp.sum(total[-EXTRA:], 0, keepdims=True)
        sent = jnp.concatenate([top, split_rows(end).astype(BF)], 0)
        mine, gots = sent.astype(F32), [hop(sent, "vox", far)]
        far *= 2
    first, corr, step, gram = call(
        fold_line,
        [
            shape((frames, LANE), BF),
            shape((frames, LANE), F32),
            shape((8, LANE), F32),
            shape((own, LANE), BF),
        ],
        (mine, *gots),
    )
    firsts = [first] + [hop(first, "vox", m) for m in line]
    grams = [gram] + [hop(gram, "frame", s) for s in range(1, n_frame)]
    odd = [hop(x, "vox", 1) for x in firsts]
    ordered = [x for pair in zip(firsts, odd) for x in pair]
    code = call(
        functools.partial(second, blocks, n_frame),
        [shape((frames, LANE), BF)],
        (*ordered, *grams, corr, step),
        [pltpu.VMEM((modes, LANE), BF)],
        2 * frames * modes * LANE,
    )
    half = call(
        pack,
        [shape((blocks // 2, frames, LANE), BF)],
        (code, *[hop(code, "vox", m) for m in line]),
    )
    batches = [hop(batch, "frame", s) for s in range(1, n_frame)]
    halves = [hop(half, "frame", s) for s in range(1, n_frame)]
    other = hop(half, "vox", 1)
    others = [hop(h, "vox", 1) for h in halves]
    codes, total = call(
        own_group,
        [shape((frames, modes), BF), shape((own, width), F32)],
        (half, other, masked, batch),
        flops=2 * frames * modes * width,
    )
    gradient = call(
        functools.partial(last_groups, n_frame - 1, 1.0 / (frames * n_frame)),
        [shape((own, width), F32)],
        (*halves, *others, *batches, masked, sup, total),
        [pltpu.VMEM((frames, modes), BF)],
        2 * (n_frame - 1) * frames * modes * width,
    )
    return codes, gradient


def solution(mesh):
    placed = (P("frame", "vox"), P(None, "vox"), P(None, "vox"), P("frame"))
    return jax.shard_map(
        body,
        mesh=mesh,
        in_specs=placed,
        out_specs=(P("frame", None), P("frame", "vox")),
        check_vma=False,
    )
```

```python
import functools

import jax
import jax.numpy as jnp
from jax import lax
from jax.experimental import pallas as pl
from jax.experimental.pallas import tpu as pltpu
from jax.sharding import PartitionSpec as P


LANE = 128
EXTRA = 16
BF = jnp.bfloat16
F32 = jnp.float32


def mm(left, right, a, b):
    return lax.dot_general(left, right, (((a,), (b,)), ((), ())), preferred_element_type=F32)


def shrink(value, limit):
    return value - jnp.clip(value, -limit, limit)


def expand_keep(sup, width):
    blocks = sup.shape[0]
    row = lax.broadcasted_iota(jnp.int32, (blocks, width), 0)
    col = lax.broadcasted_iota(jnp.int32, (blocks, width), 1)
    spread = jnp.where(col // (width // blocks) == row, 1.0, 0.0).astype(BF)
    return mm(sup.astype(F32).astype(BF), spread, 0, 0).astype(BF)


def split_rows(total):
    hi = total.astype(BF)
    rest = total - hi.astype(F32)
    mid = rest.astype(BF)
    low = (rest - mid.astype(F32)).astype(BF)
    row = lax.broadcasted_iota(jnp.int32, (EXTRA, LANE), 0)
    out = jnp.where(row == 0, hi.astype(F32), 0.0)
    out = jnp.where(row == 1, mid.astype(F32), out)
    return jnp.where(row == 2, low.astype(F32), out)


def block_of(index, size):
    return pl.ds(pl.multiple_of(index * size, size), size)


def prepare(pool, dic, sup, pick, batch, masked, keep, send, lhs):
    v, f = lax.axis_index("vox"), lax.axis_index("frame")
    frames, width = batch.shape
    modes = dic.shape[0]
    own = lhs.shape[0] - frames
    source = lax.broadcasted_iota(jnp.int32, (pool.shape[0], frames), 0)
    chosen = jnp.where(source == pick[...], 1.0, 0.0).astype(BF)
    rows = mm(chosen, pool[...], 0, 0).astype(BF)
    batch[...] = rows
    lhs[:frames, :] = rows
    for m in range(modes // LANE):
        at = slice(m * LANE, (m + 1) * LANE)
        masked[at, :] = dic[at, :] * expand_keep(sup[:, at], width)
    lhs[frames:, :] = masked[block_of(f, own), :]
    ones = jnp.ones((8, width), BF)
    for r in range(modes // LANE):
        block = masked[block_of((v % (modes // LANE)) ^ r, LANE), :]
        part = mm(lhs[...], block, 1, 1)
        square = jnp.square(block.astype(F32))
        hi = square.astype(BF)
        lo = (square - hi.astype(F32)).astype(BF)
        energy = (mm(ones, hi, 1, 1) + mm(ones, lo, 1, 1))[:1]
        height = part.shape[0]
        if r % 2:
            send[r // 2, :height, :] = part.astype(BF)
            send[r // 2, height:, :] = split_rows(energy).astype(BF)
        else:
            row = lax.broadcasted_iota(jnp.int32, (EXTRA, LANE), 0)
            keep[r // 2, :height, :] = part
            keep[r // 2, height:, :] = jnp.where(row == 0, energy, 0.0)


def fold_core(keep, got, own, *sends):
    height = own.shape[0] - EXTRA
    own[...] = keep[0] + got[0].astype(F32)
    for i, out in enumerate(sends):
        total = keep[i + 1] + got[i + 1].astype(F32)
        out[:height, :] = total[:height].astype(BF)
        out[height:, :] = split_rows(jnp.sum(total[height:], axis=0, keepdims=True)).astype(BF)


def fold_line(own, *rest):
    *gots, first, corr, step, gram = rest
    frames = first.shape[0]
    total = own[...]
    for got in gots:
        total = total + got[...].astype(F32)
    energy = jnp.sum(total[total.shape[0] - EXTRA :], axis=0, keepdims=True)
    scale = 1.0 / (energy + 1e-05)
    corr[...] = total[:frames]
    first[...] = shrink(total[:frames] * scale, 0.3 * scale).astype(BF)
    step[...] = jnp.broadcast_to(scale, step.shape)
    gram[...] = total[frames : total.shape[0] - EXTRA].astype(BF)


def second(n_first, n_gram, *refs):
    firsts = refs[:n_first]
    grams = refs[n_first : n_first + n_gram]
    corr, step, codes, square = refs[n_first + n_gram :]
    v, f = lax.axis_index("vox"), lax.axis_index("frame")
    own = grams[0].shape[0]
    for s in range(n_gram):
        square[block_of(f ^ s, own), :] = grams[s][...]
    push = -corr[...]
    for r in range(n_first):
        push = push + mm(firsts[r][...], square[block_of((v % n_first) ^ r, LANE), :], 1, 0)
    scale = step[:1, :]
    codes[...] = shrink(firsts[0][...].astype(F32) - scale * push, 0.3 * scale).astype(BF)


def pack(*refs):
    *parts, out = refs
    for i, part in enumerate(parts):
        out[i] = part[...]


def place(half, other, whole):
    v = lax.axis_index("vox")
    count = half.shape[0]
    for i in range(count):
        whole[:, block_of((v % (2 * count)) ^ (2 * i), LANE)] = half[i]
        whole[:, block_of((v % (2 * count)) ^ (2 * i + 1), LANE)] = other[i]


def own_group(half, other, masked, batch, codes, total):
    f = lax.axis_index("frame")
    place(half, other, codes)
    error = (mm(codes[...], masked[...], 1, 0) - batch[...].astype(F32)).astype(BF)
    rows = total.shape[0]
    total[...] = mm(codes[:, block_of(f, rows)], error, 0, 0)


def last_groups(n, scale, *refs):
    halves, others, batches = refs[:n], refs[n : 2 * n], refs[2 * n : 3 * n]
    masked, sup, total, gradient, codes = refs[3 * n :]
    f = lax.axis_index("frame")
    rows = total.shape[0]
    acc = total[...]
    for i in range(n):
        place(halves[i], others[i], codes)
        error = (mm(codes[...], masked[...], 1, 0) - batches[i][...].astype(F32)).astype(BF)
        acc = acc + mm(codes[:, block_of(f, rows)], error, 0, 0)
    kept = expand_keep(sup[:, block_of(f, rows)], total.shape[1]).astype(F32)
    gradient[...] = kept * acc * scale


def call(kernel, outs, args, scratch=(), flops=0):
    moved = sum(a.size * a.dtype.itemsize for a in (*args, *outs))
    single = len(outs) == 1
    return pl.pallas_call(
        kernel,
        out_shape=outs[0] if single else outs,
        in_specs=[pl.BlockSpec(memory_space=pltpu.VMEM)] * len(args),
        out_specs=pl.BlockSpec(memory_space=pltpu.VMEM)
        if single
        else [pl.BlockSpec(memory_space=pltpu.VMEM)] * len(outs),
        scratch_shapes=list(scratch),
        compiler_params=pltpu.CompilerParams(vmem_limit_bytes=8 * 2**20),
        cost_estimate=pl.CostEstimate(flops=flops, bytes_accessed=moved, transcendentals=0),
    )(*args)


def shape(dims, dtype):
    return jax.ShapeDtypeStruct(dims, dtype)


def work(pool, dictionary, support, pick):
    n_vox, n_frame = lax.axis_size("vox"), lax.axis_size("frame")
    modes, width = dictionary.shape
    frames = pick.shape[0]
    blocks = modes // LANE
    own = modes // n_frame
    height = frames + own + EXTRA
    line = [m for m in range(2, blocks, 2)]

    def hop(x, axis, m):
        n = n_vox if axis == "vox" else n_frame
        return lax.ppermute(x, axis, [(k, k ^ m) for k in range(n)])

    sup = support.T
    batch, masked, keep, send = call(
        prepare,
        [
            shape((frames, width), BF),
            shape((modes, width), BF),
            shape((blocks // 2, height, LANE), F32),
            shape((blocks // 2, height, LANE), BF),
        ],
        (pool, dictionary, sup, pick.reshape(1, frames)),
        [pltpu.VMEM((frames + own, width), BF)],
        2 * (frames + own) * modes * width,
    )
    got = hop(send, "vox", 1)
    mine, *sends = call(
        fold_core,
        [shape((height, LANE), F32)] + [shape((height, LANE), BF)] * len(line),
        (keep, got),
    )
    gots = [hop(s, "vox", m) for s, m in zip(sends, line)]
    far = blocks
    while far < n_vox:
        total = mine
        for g in gots:
            total = total + g.astype(F32)
        top, end = total[:-EXTRA].astype(BF), jnp.sum(total[-EXTRA:], 0, keepdims=True)
        sent = jnp.concatenate([top, split_rows(end).astype(BF)], 0)
        mine, gots = sent.astype(F32), [hop(sent, "vox", far)]
        far *= 2
    first, corr, step, gram = call(
        fold_line,
        [
            shape((frames, LANE), BF),
            shape((frames, LANE), F32),
            shape((8, LANE), F32),
            shape((own, LANE), BF),
        ],
        (mine, *gots),
    )
    firsts = [first] + [hop(first, "vox", m) for m in line]
    grams = [gram] + [hop(gram, "frame", s) for s in range(1, n_frame)]
    odd = [hop(x, "vox", 1) for x in firsts]
    ordered = [x for pair in zip(firsts, odd) for x in pair]
    code = call(
        functools.partial(second, blocks, n_frame),
        [shape((frames, LANE), BF)],
        (*ordered, *grams, corr, step),
        [pltpu.VMEM((modes, LANE), BF)],
        2 * frames * modes * LANE,
    )
    half = call(
        pack, [shape((blocks // 2, frames, LANE), BF)], (code, *[hop(code, "vox", m) for m in line])
    )
    batches = [hop(batch, "frame", s) for s in range(1, n_frame)]
    halves = [hop(half, "frame", s) for s in range(1, n_frame)]
    other = hop(half, "vox", 1)
    others = [hop(h, "vox", 1) for h in halves]
    codes, total = call(
        own_group,
        [shape((frames, modes), BF), shape((own, width), F32)],
        (half, other, masked, batch),
        flops=2 * frames * modes * width,
    )
    gradient = call(
        functools.partial(last_groups, n_frame - 1, 1.0 / (frames * n_frame)),
        [shape((own, width), F32)],
        (*halves, *others, *batches, masked, sup, total),
        [pltpu.VMEM((frames, modes), BF)],
        2 * (n_frame - 1) * frames * modes * width,
    )
    return codes, gradient


def solution(mesh):
    placed = (P("frame", "vox"), P(None, "vox"), P(None, "vox"), P("frame"))
    return jax.shard_map(
        work,
        mesh=mesh,
        in_specs=placed,
        out_specs=(P("frame", None), P("frame", "vox")),
        check_vma=False,
    )
```

```python
import functools

import jax
import jax.numpy as jnp
from jax import lax
from jax.experimental import pallas as pl
from jax.experimental.pallas import tpu as pltpu
from jax.sharding import PartitionSpec as P


LANE = 128
EXTRA = 16
BF = jnp.bfloat16
F32 = jnp.float32


def mm(left, right, a, b):
    return lax.dot_general(left, right, (((a,), (b,)), ((), ())), preferred_element_type=F32)


def shrink(value, limit):
    return value - jnp.clip(value, -limit, limit)


def expand_keep(sup, width):
    blocks = sup.shape[0]
    row = lax.broadcasted_iota(jnp.int32, (blocks, width), 0)
    col = lax.broadcasted_iota(jnp.int32, (blocks, width), 1)
    spread = jnp.where(col // (width // blocks) == row, 1.0, 0.0).astype(BF)
    return mm(sup.astype(F32).astype(BF), spread, 0, 0).astype(BF)


def split_rows(total):
    hi = total.astype(BF)
    rest = total - hi.astype(F32)
    mid = rest.astype(BF)
    low = (rest - mid.astype(F32)).astype(BF)
    row = lax.broadcasted_iota(jnp.int32, (EXTRA, LANE), 0)
    out = jnp.where(row == 0, hi.astype(F32), 0.0)
    out = jnp.where(row == 1, mid.astype(F32), out)
    return jnp.where(row == 2, low.astype(F32), out)


def block_of(index, size):
    return pl.ds(pl.multiple_of(index * size, size), size)


def prepare(pool_hbm, dic_hbm, sup_hbm, pick_hbm, batch, masked, keep, send, *scratch):
    pool, dic, sup, pick, sems, block_sems = scratch
    v = lax.axis_index("vox")
    frames, width = batch.shape
    blocks = dic.shape[0] // LANE
    copies = [
        pltpu.make_async_copy(source, target, sems.at[i])
        for i, (source, target) in enumerate([(pick_hbm, pick), (sup_hbm, sup), (pool_hbm, pool)])
    ]
    spots = [block_of((v % blocks) ^ r, LANE) for r in range(blocks)]
    parts = [
        pltpu.make_async_copy(dic_hbm.at[at, :], dic.at[at, :], block_sems.at[r])
        for r, at in enumerate(spots)
    ]
    for copy in copies + parts:
        copy.start()
    for copy in copies:
        copy.wait()
    source = lax.broadcasted_iota(jnp.int32, (pool.shape[0], frames), 0)
    chosen = jnp.where(source == pick[...], 1.0, 0.0).astype(BF)
    batch[...] = mm(chosen, pool[...], 0, 0).astype(BF)
    ones = jnp.ones((8, LANE), BF)
    row = lax.broadcasted_iota(jnp.int32, (EXTRA, LANE), 0)
    for i in range(blocks // 2):
        pair = []
        for r in (2 * i, 2 * i + 1):
            parts[r].wait()
            block = dic[spots[r], :] * expand_keep(sup[:, spots[r]], width)
            masked[spots[r], :] = block
            pair.append(block)
        part = mm(batch[...], jnp.concatenate(pair, axis=0), 1, 1)
        keep[i, :frames, :] = part[:, :LANE]
        send[i, :frames, :] = part[:, LANE:].astype(BF)
        for block, out in zip(pair, (keep, send)):
            square = jnp.square(block.astype(F32))
            folded = square[:, :LANE]
            for j in range(1, width // LANE):
                folded = folded + square[:, j * LANE : (j + 1) * LANE]
            hi = folded.astype(BF)
            rest = folded - hi.astype(F32)
            mid = rest.astype(BF)
            low = (rest - mid.astype(F32)).astype(BF)
            energy = (mm(ones, hi, 1, 1) + (mm(ones, mid, 1, 1) + mm(ones, low, 1, 1)))[:1]
            if out is keep:
                out[i, frames:, :] = jnp.where(row == 0, energy, 0.0)
            else:
                out[i, frames:, :] = split_rows(energy).astype(BF)


def gram_part(masked, keep, send):
    v, f = lax.axis_index("vox"), lax.axis_index("frame")
    own = keep.shape[1]
    blocks = masked.shape[0] // LANE
    left = masked[block_of(f, own), :]
    for i in range(blocks // 2):
        pair = [masked[block_of((v % blocks) ^ r, LANE), :] for r in (2 * i, 2 * i + 1)]
        part = mm(left, jnp.concatenate(pair, axis=0), 1, 1)
        keep[i] = part[:, :LANE]
        send[i] = part[:, LANE:].astype(BF)


def pack_sum(total, extra):
    if not extra:
        return total.astype(BF)
    top = total.shape[0] - extra
    energy = jnp.sum(total[top:], axis=0, keepdims=True)
    return jnp.concatenate([total[:top].astype(BF), split_rows(energy).astype(BF)], axis=0)


def fold_core(extra, keep, got, own, *sends):
    own[...] = keep[0] + got[0].astype(F32)
    for i, out in enumerate(sends):
        out[...] = pack_sum(keep[i + 1] + got[i + 1].astype(F32), extra)


def fold_line(own, *rest):
    *gots, first, corr, step = rest
    frames = first.shape[0]
    total = own[...]
    for got in gots:
        total = total + got[...].astype(F32)
    energy = jnp.sum(total[frames:], axis=0, keepdims=True)
    scale = 1.0 / (energy + 1e-05)
    corr[...] = total[:frames]
    first[...] = shrink(total[:frames] * scale, 0.3 * scale).astype(BF)
    step[...] = jnp.broadcast_to(scale, step.shape)


def fold_gram(own, *rest):
    *gots, gram = rest
    total = own[...]
    for got in gots:
        total = total + got[...].astype(F32)
    gram[...] = total.astype(BF)


def second(n_first, n_gram, *refs):
    firsts = refs[:n_first]
    grams = refs[n_first : n_first + n_gram]
    corr, step, codes, square = refs[n_first + n_gram :]
    v, f = lax.axis_index("vox"), lax.axis_index("frame")
    own = grams[0].shape[0]
    for s in range(n_gram):
        square[block_of(f ^ s, own), :] = grams[s][...]
    push = -corr[...]
    for r in range(n_first):
        push = push + mm(firsts[r][...], square[block_of((v % n_first) ^ r, LANE), :], 1, 0)
    scale = step[:1, :]
    codes[...] = shrink(firsts[0][...].astype(F32) - scale * push, 0.3 * scale).astype(BF)


def pack(*refs):
    *parts, out = refs
    for i, part in enumerate(parts):
        out[i] = part[...]


def place(half, other, whole):
    v = lax.axis_index("vox")
    count = half.shape[0]
    for i in range(count):
        whole[:, block_of((v % (2 * count)) ^ (2 * i), LANE)] = half[i]
        whole[:, block_of((v % (2 * count)) ^ (2 * i + 1), LANE)] = other[i]


def own_group(half, other, masked, batch, codes, total):
    f = lax.axis_index("frame")
    place(half, other, codes)
    error = (mm(codes[...], masked[...], 1, 0) - batch[...].astype(F32)).astype(BF)
    rows = total.shape[0]
    total[...] = mm(codes[:, block_of(f, rows)], error, 0, 0)


def add_group(half, other, batch, masked, total, out, codes):
    f = lax.axis_index("frame")
    place(half, other, codes)
    error = (mm(codes[...], masked[...], 1, 0) - batch[...].astype(F32)).astype(BF)
    out[...] = total[...] + mm(codes[:, block_of(f, total.shape[0])], error, 0, 0)


def last_group(scale, half, other, batch, masked, total, sup, out, codes):
    f = lax.axis_index("frame")
    add_group(half, other, batch, masked, total, out, codes)
    kept = expand_keep(sup[:, block_of(f, total.shape[0])], total.shape[1]).astype(F32)
    out[...] = kept * out[...] * scale


def call(kernel, outs, args, scratch=(), flops=0, space=pltpu.VMEM):
    moved = sum(a.size * a.dtype.itemsize for a in (*args, *outs))
    single = len(outs) == 1
    return pl.pallas_call(
        kernel,
        out_shape=outs[0] if single else outs,
        in_specs=[pl.BlockSpec(memory_space=space)] * len(args),
        out_specs=pl.BlockSpec(memory_space=pltpu.VMEM)
        if single
        else [pl.BlockSpec(memory_space=pltpu.VMEM)] * len(outs),
        scratch_shapes=list(scratch),
        compiler_params=pltpu.CompilerParams(vmem_limit_bytes=8 * 2**20),
        cost_estimate=pl.CostEstimate(flops=flops, bytes_accessed=moved, transcendentals=0),
    )(*args)


def shape(dims, dtype):
    return jax.ShapeDtypeStruct(dims, dtype)


def work(pool, dictionary, support, pick):
    n_vox, n_frame = lax.axis_size("vox"), lax.axis_size("frame")
    modes, width = dictionary.shape
    frames = pick.shape[0]
    blocks = modes // LANE
    own = modes // n_frame
    line = [m for m in range(2, blocks, 2)]

    def hop(x, axis, m):
        n = n_vox if axis == "vox" else n_frame
        return lax.ppermute(x, axis, [(k, k ^ m) for k in range(n)])

    def reduce(keep, send, extra):
        tall = keep.shape[1]
        got = hop(send, "vox", 1)
        mine, *sends = call(
            functools.partial(fold_core, extra),
            [shape((tall, LANE), F32)] + [shape((tall, LANE), BF)] * len(line),
            (keep, got),
        )
        gots = [hop(s, "vox", m) for s, m in zip(sends, line)]
        far = blocks
        while far < n_vox:
            total = mine
            for g in gots:
                total = total + g.astype(F32)
            sent = pack_sum(total, extra)
            mine, gots = sent.astype(F32), [hop(sent, "vox", far)]
            far *= 2
        return mine, gots

    sup = support.T
    batch, masked, keep, send = call(
        prepare,
        [
            shape((frames, width), BF),
            shape((modes, width), BF),
            shape((blocks // 2, frames + EXTRA, LANE), F32),
            shape((blocks // 2, frames + EXTRA, LANE), BF),
        ],
        (pool, dictionary, sup, pick.reshape(1, frames)),
        [
            pltpu.VMEM(pool.shape, BF),
            pltpu.VMEM(dictionary.shape, BF),
            pltpu.VMEM(sup.shape, jnp.int32),
            pltpu.VMEM((1, frames), jnp.int32),
            pltpu.SemaphoreType.DMA((3,)),
            pltpu.SemaphoreType.DMA((blocks,)),
        ],
        2 * frames * modes * width,
        pltpu.HBM,
    )
    gram_keep, gram_send = call(
        gram_part,
        [
            shape((blocks // 2, own, LANE), F32),
            shape((blocks // 2, own, LANE), BF),
        ],
        (masked,),
        flops=2 * own * modes * width,
    )
    mine, gots = reduce(keep, send, EXTRA)
    first, corr, step = call(
        fold_line,
        [
            shape((frames, LANE), BF),
            shape((frames, LANE), F32),
            shape((8, LANE), F32),
        ],
        (mine, *gots),
    )
    mine, gots = reduce(gram_keep, gram_send, 0)
    gram = call(fold_gram, [shape((own, LANE), BF)], (mine, *gots))
    firsts = [first] + [hop(first, "vox", m) for m in line]
    grams = [gram] + [hop(gram, "frame", s) for s in range(1, n_frame)]
    odd = [hop(first, "vox", 1)] + [hop(x, "vox", 1) for x in firsts[1:]]
    ordered = [x for pair in zip(firsts, odd) for x in pair]
    code = call(
        functools.partial(second, blocks, n_frame),
        [shape((frames, LANE), BF)],
        (*ordered, *grams, corr, step),
        [pltpu.VMEM((modes, LANE), BF)],
        2 * frames * modes * LANE,
    )
    half = call(
        pack, [shape((blocks // 2, frames, LANE), BF)], (code, *[hop(code, "vox", m) for m in line])
    )
    groups = range(1, n_frame)
    batches = [hop(batch, "frame", s) for s in groups]
    halves = [hop(half, "frame", s) for s in groups]
    other = hop(half, "vox", 1)
    others = [hop(h, "vox", 1) for h in halves]
    codes, total = call(
        own_group,
        [shape((frames, modes), BF), shape((own, width), F32)],
        (half, other, masked, batch),
        flops=2 * frames * modes * width,
    )
    held = [pltpu.VMEM((frames, modes), BF)]
    work_size = 2 * frames * (modes + own) * width
    for i in range(n_frame - 1):
        args = (halves[i], others[i], batches[i], masked, total)
        if i < n_frame - 2:
            total = call(add_group, [shape((own, width), F32)], args, held, work_size)
        else:
            total = call(
                functools.partial(last_group, 1.0 / (frames * n_frame)),
                [shape((own, width), F32)],
                (*args, sup),
                held,
                work_size,
            )
    return codes, total


def solution(mesh):
    placed = (P("frame", "vox"), P(None, "vox"), P(None, "vox"), P("frame"))
    return jax.shard_map(
        work,
        mesh=mesh,
        in_specs=placed,
        out_specs=(P("frame", None), P("frame", "vox")),
        check_vma=False,
    )
```

```python
import functools

import jax
import jax.numpy as jnp
from jax import lax
from jax.experimental import pallas as pl
from jax.experimental.pallas import tpu as pltpu
from jax.sharding import PartitionSpec as P


LANE = 128
EXTRA = 16
BF = jnp.bfloat16
F32 = jnp.float32


def mm(left, right, a, b):
    return lax.dot_general(left, right, (((a,), (b,)), ((), ())), preferred_element_type=F32)


def shrink(value, limit):
    return value - jnp.clip(value, -limit, limit)


def expand_keep(sup, width):
    blocks = sup.shape[0]
    row = lax.broadcasted_iota(jnp.int32, (blocks, width), 0)
    col = lax.broadcasted_iota(jnp.int32, (blocks, width), 1)
    spread = jnp.where(col // (width // blocks) == row, 1.0, 0.0).astype(BF)
    return mm(sup.astype(F32).astype(BF), spread, 0, 0).astype(BF)


def split_rows(total):
    hi = total.astype(BF)
    rest = total - hi.astype(F32)
    mid = rest.astype(BF)
    low = (rest - mid.astype(F32)).astype(BF)
    row = lax.broadcasted_iota(jnp.int32, (EXTRA, LANE), 0)
    out = jnp.where(row == 0, hi.astype(F32), 0.0)
    out = jnp.where(row == 1, mid.astype(F32), out)
    return jnp.where(row == 2, low.astype(F32), out)


def block_of(index, size):
    return pl.ds(pl.multiple_of(index * size, size), size)


def load(pool_hbm, dic_hbm, sup_hbm, pick_hbm, batch, dic, sup, pool, pick, sems):
    frames = batch.shape[0]
    pairs = [(pick_hbm, pick), (pool_hbm, pool), (sup_hbm, sup), (dic_hbm, dic)]
    copies = [pltpu.make_async_copy(a, b, sems.at[i]) for i, (a, b) in enumerate(pairs)]
    for copy in copies:
        copy.start()
    copies[0].wait()
    source = lax.broadcasted_iota(jnp.int32, (pool.shape[0], frames), 0)
    chosen = jnp.where(source == pick[...], 1.0, 0.0).astype(BF)
    copies[1].wait()
    batch[...] = mm(chosen, pool[...], 0, 0).astype(BF)
    copies[2].wait()
    copies[3].wait()


def blocks_of(odd, dic, sup, batch, masked, out):
    v = lax.axis_index("vox")
    frames, width = batch.shape
    blocks = dic.shape[0] // LANE
    ones = jnp.ones((8, LANE), BF)
    row = lax.broadcasted_iota(jnp.int32, (EXTRA, LANE), 0)
    for i in range(0, blocks // 2, 2):
        pair = []
        for r in (2 * i + odd, 2 * i + 2 + odd):
            at = block_of((v % blocks) ^ r, LANE)
            block = dic[at, :] * expand_keep(sup[:, at], width)
            masked[at, :] = block
            pair.append(block)
        part = mm(batch[...], jnp.concatenate(pair, axis=0), 1, 1)
        for j, block in enumerate(pair):
            out[i + j, :frames, :] = part[:, j * LANE : (j + 1) * LANE].astype(out.dtype)
            square = jnp.square(block.astype(F32))
            folded = square[:, :LANE]
            for k in range(1, width // LANE):
                folded = folded + square[:, k * LANE : (k + 1) * LANE]
            hi = folded.astype(BF)
            rest = folded - hi.astype(F32)
            mid = rest.astype(BF)
            low = (rest - mid.astype(F32)).astype(BF)
            energy = (mm(ones, hi, 1, 1) + (mm(ones, mid, 1, 1) + mm(ones, low, 1, 1)))[:1]
            if odd:
                out[i + j, frames:, :] = split_rows(energy).astype(BF)
            else:
                out[i + j, frames:, :] = jnp.where(row == 0, energy, 0.0)


def send_part(dic, sup, batch, masked, send):
    blocks_of(1, dic, sup, batch, masked, send)


def keep_part(dic, sup, batch, half, masked, keep):
    blocks_of(0, dic, sup, batch, masked, keep)


def gram_part(masked, keep, send):
    v, f = lax.axis_index("vox"), lax.axis_index("frame")
    own = keep.shape[1]
    blocks = masked.shape[0] // LANE
    left = masked[block_of(f, own), :]
    for i in range(blocks // 2):
        pair = [masked[block_of((v % blocks) ^ r, LANE), :] for r in (2 * i, 2 * i + 1)]
        part = mm(left, jnp.concatenate(pair, axis=0), 1, 1)
        keep[i] = part[:, :LANE]
        send[i] = part[:, LANE:].astype(BF)


def pack_sum(total, extra):
    if not extra:
        return total.astype(BF)
    top = total.shape[0] - extra
    energy = jnp.sum(total[top:], axis=0, keepdims=True)
    return jnp.concatenate([total[:top].astype(BF), split_rows(energy).astype(BF)], axis=0)


def fold_core(extra, keep, got, own, *sends):
    own[...] = keep[0] + got[0].astype(F32)
    for i, out in enumerate(sends):
        out[...] = pack_sum(keep[i + 1] + got[i + 1].astype(F32), extra)


def fold_line(own, *rest):
    *gots, first, corr, step = rest
    frames = first.shape[0]
    total = own[...]
    for got in gots:
        total = total + got[...].astype(F32)
    energy = jnp.sum(total[frames:], axis=0, keepdims=True)
    scale = 1.0 / (energy + 1e-05)
    corr[...] = total[:frames]
    first[...] = shrink(total[:frames] * scale, 0.3 * scale).astype(BF)
    step[...] = jnp.broadcast_to(scale, step.shape)


def fold_gram(own, *rest):
    *gots, gram = rest
    total = own[...]
    for got in gots:
        total = total + got[...].astype(F32)
    gram[...] = total.astype(BF)


def second(n_first, n_gram, *refs):
    firsts = refs[:n_first]
    grams = refs[n_first : n_first + n_gram]
    corr, step, codes, square = refs[n_first + n_gram :]
    v, f = lax.axis_index("vox"), lax.axis_index("frame")
    own = grams[0].shape[0]
    for s in range(n_gram):
        square[block_of(f ^ s, own), :] = grams[s][...]
    push = -corr[...]
    for r in range(n_first):
        push = push + mm(firsts[r][...], square[block_of((v % n_first) ^ r, LANE), :], 1, 0)
    scale = step[:1, :]
    codes[...] = shrink(firsts[0][...].astype(F32) - scale * push, 0.3 * scale).astype(BF)


def pack(*refs):
    *parts, half, rest = refs
    for i, part in enumerate(parts):
        half[i] = part[...]
        if i:
            rest[i - 1] = part[...]


def join(own, rest, half):
    half[0] = own[...]
    half[1:] = rest[...]


def place(half, other, whole):
    v = lax.axis_index("vox")
    count = half.shape[0]
    for i in range(count):
        whole[:, block_of((v % (2 * count)) ^ (2 * i), LANE)] = half[i]
        whole[:, block_of((v % (2 * count)) ^ (2 * i + 1), LANE)] = other[i]


def own_group(half, other, masked, batch, codes, total):
    f = lax.axis_index("frame")
    place(half, other, codes)
    error = (mm(codes[...], masked[...], 1, 0) - batch[...].astype(F32)).astype(BF)
    rows = total.shape[0]
    total[...] = mm(codes[:, block_of(f, rows)], error, 0, 0)


def add_group(half, other, batch, masked, total, out, codes):
    f = lax.axis_index("frame")
    place(half, other, codes)
    error = (mm(codes[...], masked[...], 1, 0) - batch[...].astype(F32)).astype(BF)
    out[...] = total[...] + mm(codes[:, block_of(f, total.shape[0])], error, 0, 0)


def last_group(scale, half, other, batch, masked, total, sup, out, codes):
    f = lax.axis_index("frame")
    add_group(half, other, batch, masked, total, out, codes)
    kept = expand_keep(sup[:, block_of(f, total.shape[0])], total.shape[1]).astype(F32)
    out[...] = kept * out[...] * scale


def call(kernel, outs, args, scratch=(), flops=0, space=pltpu.VMEM, alias=None):
    moved = sum(a.size * a.dtype.itemsize for a in (*args, *outs))
    single = len(outs) == 1
    return pl.pallas_call(
        kernel,
        out_shape=outs[0] if single else outs,
        in_specs=[pl.BlockSpec(memory_space=space)] * len(args),
        out_specs=pl.BlockSpec(memory_space=pltpu.VMEM)
        if single
        else [pl.BlockSpec(memory_space=pltpu.VMEM)] * len(outs),
        scratch_shapes=list(scratch),
        input_output_aliases=alias or {},
        compiler_params=pltpu.CompilerParams(vmem_limit_bytes=8 * 2**20),
        cost_estimate=pl.CostEstimate(flops=flops, bytes_accessed=moved, transcendentals=0),
    )(*args)


def shape(dims, dtype):
    return jax.ShapeDtypeStruct(dims, dtype)


def work(pool, dictionary, support, pick):
    n_vox, n_frame = lax.axis_size("vox"), lax.axis_size("frame")
    modes, width = dictionary.shape
    frames = pick.shape[0]
    blocks = modes // LANE
    own = modes // n_frame
    line = [m for m in range(2, blocks, 2)]

    def hop(x, axis, m):
        n = n_vox if axis == "vox" else n_frame
        return lax.ppermute(x, axis, [(k, k ^ m) for k in range(n)])

    def reduce(keep, send, extra):
        tall = keep.shape[1]
        got = hop(send, "vox", 1)
        mine, *sends = call(
            functools.partial(fold_core, extra),
            [shape((tall, LANE), F32)] + [shape((tall, LANE), BF)] * len(line),
            (keep, got),
        )
        gots = [hop(s, "vox", m) for s, m in zip(sends, line)]
        far = blocks
        while far < n_vox:
            total = mine
            for g in gots:
                total = total + g.astype(F32)
            sent = pack_sum(total, extra)
            mine, gots = sent.astype(F32), [hop(sent, "vox", far)]
            far *= 2
        return mine, gots

    sup = support.T
    raw = (pool, dictionary, sup, pick.reshape(1, frames))
    batch, dic, sup = call(
        load,
        [shape((frames, width), BF), shape((modes, width), BF), shape(sup.shape, jnp.int32)],
        tuple(pltpu.with_memory_space_constraint(x, pltpu.HBM) for x in raw),
        [
            pltpu.VMEM(pool.shape, BF),
            pltpu.VMEM((1, frames), jnp.int32),
            pltpu.SemaphoreType.DMA((4,)),
        ],
        2 * frames * pool.shape[0] * width,
        pltpu.HBM,
    )
    groups = range(1, n_frame)
    batches = [hop(batch, "frame", s) for s in groups]
    half_size = frames * modes * width
    part = shape((blocks // 2, frames + EXTRA, LANE), F32)
    masked, send = call(
        send_part,
        [shape((modes, width), BF), shape(part.shape, BF)],
        (dic, sup, batch),
        flops=half_size,
    )
    masked, keep = call(
        keep_part,
        [shape((modes, width), BF), part],
        (dic, sup, batch, masked),
        flops=half_size,
        alias={3: 0},
    )
    gram_keep, gram_send = call(
        gram_part,
        [
            shape((blocks // 2, own, LANE), F32),
            shape((blocks // 2, own, LANE), BF),
        ],
        (masked,),
        flops=2 * own * modes * width,
    )
    mine, gots = reduce(keep, send, EXTRA)
    first, corr, step = call(
        fold_line,
        [
            shape((frames, LANE), BF),
            shape((frames, LANE), F32),
            shape((8, LANE), F32),
        ],
        (mine, *gots),
    )
    mine, gots = reduce(gram_keep, gram_send, 0)
    gram = call(fold_gram, [shape((own, LANE), BF)], (mine, *gots))
    firsts = [first] + [hop(first, "vox", m) for m in line]
    grams = [gram] + [hop(gram, "frame", s) for s in range(1, n_frame)]
    odd = [hop(first, "vox", 1)] + [hop(x, "vox", 1) for x in firsts[1:]]
    ordered = [x for pair in zip(firsts, odd) for x in pair]
    code = call(
        functools.partial(second, blocks, n_frame),
        [shape((frames, LANE), BF)],
        (*ordered, *grams, corr, step),
        [pltpu.VMEM((modes, LANE), BF)],
        2 * frames * modes * LANE,
    )
    own_hops = [hop(code, "frame", s) for s in groups]
    half, rest = call(
        pack,
        [shape((blocks // 2, frames, LANE), BF), shape((blocks // 2 - 1, frames, LANE), BF)],
        (code, *[hop(code, "vox", m) for m in line]),
    )
    halves = [call(join, [half], (o, hop(rest, "frame", s))) for s, o in zip(groups, own_hops)]
    other = hop(half, "vox", 1)
    others = [hop(h, "vox", 1) for h in halves]
    codes, total = call(
        own_group,
        [shape((frames, modes), BF), shape((own, width), F32)],
        (half, other, masked, batch),
        flops=2 * frames * modes * width,
    )
    held = [pltpu.VMEM((frames, modes), BF)]
    work_size = 2 * frames * (modes + own) * width
    for i in range(n_frame - 1):
        args = (halves[i], others[i], batches[i], masked, total)
        if i < n_frame - 2:
            total = call(add_group, [shape((own, width), F32)], args, held, work_size)
        else:
            total = call(
                functools.partial(last_group, 1.0 / (frames * n_frame)),
                [shape((own, width), F32)],
                (*args, sup),
                held,
                work_size,
            )
    return codes, total


def solution(mesh):
    placed = (P("frame", "vox"), P(None, "vox"), P(None, "vox"), P("frame"))
    return jax.shard_map(
        work,
        mesh=mesh,
        in_specs=placed,
        out_specs=(P("frame", None), P("frame", "vox")),
        check_vma=False,
    )
```

```python
import functools

import jax
import jax.numpy as jnp
from jax import lax
from jax.experimental import pallas as pl
from jax.experimental.pallas import tpu as pltpu
from jax.sharding import PartitionSpec as P


LANE = 128
EXTRA = 16
BF = jnp.bfloat16
F32 = jnp.float32


def mm(left, right, a, b):
    return lax.dot_general(left, right, (((a,), (b,)), ((), ())), preferred_element_type=F32)


def shrink(value, limit):
    return value - jnp.clip(value, -limit, limit)


def expand_keep(sup, width):
    blocks = sup.shape[0]
    row = lax.broadcasted_iota(jnp.int32, (blocks, width), 0)
    col = lax.broadcasted_iota(jnp.int32, (blocks, width), 1)
    spread = jnp.where(col // (width // blocks) == row, 1.0, 0.0).astype(BF)
    return mm(sup.astype(F32).astype(BF), spread, 0, 0).astype(BF)


def split_rows(total):
    hi = total.astype(BF)
    rest = total - hi.astype(F32)
    mid = rest.astype(BF)
    low = (rest - mid.astype(F32)).astype(BF)
    row = lax.broadcasted_iota(jnp.int32, (EXTRA, LANE), 0)
    out = jnp.where(row == 0, hi.astype(F32), 0.0)
    out = jnp.where(row == 1, mid.astype(F32), out)
    return jnp.where(row == 2, low.astype(F32), out)


def block_of(index, size):
    return pl.ds(pl.multiple_of(index * size, size), size)


def load(pool_hbm, dic_hbm, sup_hbm, pick_hbm, batch, dic, sup, pool, pick, sems):
    frames = batch.shape[0]
    pairs = [(pick_hbm, pick), (pool_hbm, pool), (sup_hbm, sup), (dic_hbm, dic)]
    copies = [pltpu.make_async_copy(a, b, sems.at[i]) for i, (a, b) in enumerate(pairs)]
    for copy in copies:
        copy.start()
    copies[0].wait()
    source = lax.broadcasted_iota(jnp.int32, (pool.shape[0], frames), 0)
    chosen = jnp.where(source == pick[...], 1.0, 0.0).astype(BF)
    copies[1].wait()
    batch[...] = mm(chosen, pool[...], 0, 0).astype(BF)
    copies[2].wait()
    copies[3].wait()


def blocks_of(odd, dic, sup, batch, masked, out):
    v = lax.axis_index("vox")
    frames, width = batch.shape
    blocks = dic.shape[0] // LANE
    ones = jnp.ones((8, LANE), BF)
    row = lax.broadcasted_iota(jnp.int32, (EXTRA, LANE), 0)
    for i in range(0, blocks // 2, 2):
        pair = []
        for r in (2 * i + odd, 2 * i + 2 + odd):
            at = block_of((v % blocks) ^ r, LANE)
            block = dic[at, :] * expand_keep(sup[:, at], width)
            masked[at, :] = block
            pair.append(block)
        part = mm(batch[...], jnp.concatenate(pair, axis=0), 1, 1)
        for j, block in enumerate(pair):
            out[i + j, :frames, :] = part[:, j * LANE : (j + 1) * LANE].astype(out.dtype)
            square = jnp.square(block.astype(F32))
            folded = square[:, :LANE]
            for k in range(1, width // LANE):
                folded = folded + square[:, k * LANE : (k + 1) * LANE]
            hi = folded.astype(BF)
            rest = folded - hi.astype(F32)
            mid = rest.astype(BF)
            low = (rest - mid.astype(F32)).astype(BF)
            energy = (mm(ones, hi, 1, 1) + (mm(ones, mid, 1, 1) + mm(ones, low, 1, 1)))[:1]
            if odd:
                out[i + j, frames:, :] = split_rows(energy).astype(BF)
            else:
                out[i + j, frames:, :] = jnp.where(row == 0, energy, 0.0)


def send_part(dic, sup, batch, masked, send):
    blocks_of(1, dic, sup, batch, masked, send)


def keep_part(dic, sup, batch, half, masked, keep):
    blocks_of(0, dic, sup, batch, masked, keep)


def gram_part(masked, keep, send):
    v, f = lax.axis_index("vox"), lax.axis_index("frame")
    own = keep.shape[1]
    blocks = masked.shape[0] // LANE
    left = masked[block_of(f, own), :]
    for i in range(blocks // 2):
        pair = [masked[block_of((v % blocks) ^ r, LANE), :] for r in (2 * i, 2 * i + 1)]
        part = mm(left, jnp.concatenate(pair, axis=0), 1, 1)
        keep[i] = part[:, :LANE]
        send[i] = part[:, LANE:].astype(BF)


def pack_sum(total, extra):
    if not extra:
        return total.astype(BF)
    top = total.shape[0] - extra
    energy = jnp.sum(total[top:], axis=0, keepdims=True)
    return jnp.concatenate([total[:top].astype(BF), split_rows(energy).astype(BF)], axis=0)


def fold_core(keep, got, own, *sends):
    own[...] = keep[0] + got[0].astype(F32)
    for i, out in enumerate(sends):
        out[...] = pack_sum(keep[i + 1] + got[i + 1].astype(F32), EXTRA)


def fold_half(keep, got, left, sent):
    for i in range(keep.shape[0]):
        total = keep[i] + got[i].astype(F32)
        if i % 2:
            sent[i // 2] = total.astype(BF)
        else:
            left[i // 2] = total


def fold_line(own, *rest):
    *gots, first, corr, step = rest
    frames = first.shape[0]
    total = own[...]
    for got in gots:
        total = total + got[...].astype(F32)
    energy = jnp.sum(total[frames:], axis=0, keepdims=True)
    scale = 1.0 / (energy + 1e-05)
    corr[...] = total[:frames]
    first[...] = shrink(total[:frames] * scale, 0.3 * scale).astype(BF)
    step[...] = jnp.broadcast_to(scale, step.shape)


def fold_gram(own, *rest):
    *gots, gram = rest
    total = own[...]
    for got in gots:
        total = total + got[...].astype(F32)
    gram[...] = total.astype(BF)


def second(n_first, n_gram, *refs):
    firsts = refs[:n_first]
    grams = refs[n_first : n_first + n_gram]
    corr, step, codes, square = refs[n_first + n_gram :]
    v, f = lax.axis_index("vox"), lax.axis_index("frame")
    own = grams[0].shape[0]
    for s in range(n_gram):
        square[block_of(f ^ s, own), :] = grams[s][...]
    push = -corr[...]
    for r in range(n_first):
        push = push + mm(firsts[r][...], square[block_of((v % n_first) ^ r, LANE), :], 1, 0)
    scale = step[:1, :]
    codes[...] = shrink(firsts[0][...].astype(F32) - scale * push, 0.3 * scale).astype(BF)


def pack(*refs):
    *parts, half, rest = refs
    for i, part in enumerate(parts):
        half[i] = part[...]
        if i:
            rest[i - 1] = part[...]


def join(own, rest, half):
    half[0] = own[...]
    half[1:] = rest[...]


def place(half, other, whole):
    v = lax.axis_index("vox")
    count = half.shape[0]
    for i in range(count):
        whole[:, block_of((v % (2 * count)) ^ (2 * i), LANE)] = half[i]
        whole[:, block_of((v % (2 * count)) ^ (2 * i + 1), LANE)] = other[i]


def own_group(half, other, masked, batch, sup, codes, total, kept):
    f = lax.axis_index("frame")
    place(half, other, codes)
    error = (mm(codes[...], masked[...], 1, 0) - batch[...].astype(F32)).astype(BF)
    rows = total.shape[0]
    total[...] = mm(codes[:, block_of(f, rows)], error, 0, 0)
    kept[...] = expand_keep(sup[:, block_of(f, rows)], total.shape[1])


def add_group(half, other, batch, masked, total, out, codes):
    f = lax.axis_index("frame")
    place(half, other, codes)
    error = (mm(codes[...], masked[...], 1, 0) - batch[...].astype(F32)).astype(BF)
    out[...] = total[...] + mm(codes[:, block_of(f, total.shape[0])], error, 0, 0)


def last_group(scale, half, other, batch, masked, total, kept, out_hbm, codes, out, sems):
    f = lax.axis_index("frame")
    place(half, other, codes)
    rows, width = total.shape
    step = width // sems.shape[0]
    copies = []
    for i in range(sems.shape[0]):
        at = slice(i * step, (i + 1) * step)
        error = (mm(codes[...], masked[:, at], 1, 0) - batch[:, at].astype(F32)).astype(BF)
        acc = total[:, at] + mm(codes[:, block_of(f, rows)], error, 0, 0)
        out[:, at] = kept[:, at].astype(F32) * acc * scale
        copies.append(pltpu.make_async_copy(out.at[:, at], out_hbm.at[:, at], sems.at[i]))
        copies[-1].start()
    for copy in copies:
        copy.wait()


def call(kernel, outs, args, scratch=(), flops=0, space=pltpu.VMEM, alias=None, to=pltpu.VMEM):
    moved = sum(a.size * a.dtype.itemsize for a in (*args, *outs))
    single = len(outs) == 1
    return pl.pallas_call(
        kernel,
        out_shape=outs[0] if single else outs,
        in_specs=[pl.BlockSpec(memory_space=space)] * len(args),
        out_specs=pl.BlockSpec(memory_space=to)
        if single
        else [pl.BlockSpec(memory_space=to)] * len(outs),
        scratch_shapes=list(scratch),
        input_output_aliases=alias or {},
        compiler_params=pltpu.CompilerParams(vmem_limit_bytes=8 * 2**20),
        cost_estimate=pl.CostEstimate(flops=flops, bytes_accessed=moved, transcendentals=0),
    )(*args)


def shape(dims, dtype):
    return jax.ShapeDtypeStruct(dims, dtype)


def work(pool, dictionary, support, pick):
    n_vox, n_frame = lax.axis_size("vox"), lax.axis_size("frame")
    modes, width = dictionary.shape
    frames = pick.shape[0]
    blocks = modes // LANE
    own = modes // n_frame
    line = [m for m in range(2, blocks, 2)]

    def hop(x, axis, m):
        n = n_vox if axis == "vox" else n_frame
        return lax.ppermute(x, axis, [(k, k ^ m) for k in range(n)])

    def across(mine, gots, extra):
        far = blocks
        while far < n_vox:
            total = mine
            for g in gots:
                total = total + g.astype(F32)
            sent = pack_sum(total, extra)
            mine, gots = sent.astype(F32), [hop(sent, "vox", far)]
            far *= 2
        return mine, gots

    sup = support.T
    raw = (pool, dictionary, sup, pick.reshape(1, frames))
    batch, dic, sup = call(
        load,
        [shape((frames, width), BF), shape((modes, width), BF), shape(sup.shape, jnp.int32)],
        tuple(pltpu.with_memory_space_constraint(x, pltpu.HBM) for x in raw),
        [
            pltpu.VMEM(pool.shape, BF),
            pltpu.VMEM((1, frames), jnp.int32),
            pltpu.SemaphoreType.DMA((4,)),
        ],
        2 * frames * pool.shape[0] * width,
        pltpu.HBM,
    )
    groups = range(1, n_frame)
    batches = [hop(batch, "frame", s) for s in groups]
    half_size = frames * modes * width
    part = shape((blocks // 2, frames + EXTRA, LANE), F32)
    masked, send = call(
        send_part,
        [shape((modes, width), BF), shape(part.shape, BF)],
        (dic, sup, batch),
        flops=half_size,
    )
    masked, keep = call(
        keep_part,
        [shape((modes, width), BF), part],
        (dic, sup, batch, masked),
        flops=half_size,
        alias={3: 0},
    )
    gram_keep, gram_send = call(
        gram_part,
        [
            shape((blocks // 2, own, LANE), F32),
            shape((blocks // 2, own, LANE), BF),
        ],
        (masked,),
        flops=2 * own * modes * width,
    )
    tall = frames + EXTRA
    mine, *sends = call(
        fold_core,
        [shape((tall, LANE), F32)] + [shape((tall, LANE), BF)] * len(line),
        (keep, hop(send, "vox", 1)),
    )
    gots = [hop(s, "vox", m) for s, m in zip(sends, line)]
    mine, gots = across(mine, gots, EXTRA)
    first, corr, step = call(
        fold_line,
        [
            shape((frames, LANE), BF),
            shape((frames, LANE), F32),
            shape((8, LANE), F32),
        ],
        (mine, *gots),
    )
    mask = 1
    while gram_keep.shape[0] > 1:
        some = (gram_keep.shape[0] // 2, own, LANE)
        gram_keep, gram_send = call(
            fold_half, [shape(some, F32), shape(some, BF)], (gram_keep, hop(gram_send, "vox", mask))
        )
        mask *= 2
    gots = [hop(gram_send[0], "vox", mask)]
    mine, gots = across(gram_keep[0], gots, 0)
    gram = call(fold_gram, [shape((own, LANE), BF)], (mine, *gots))
    firsts = [first] + [hop(first, "vox", m) for m in line]
    grams = [gram] + [hop(gram, "frame", s) for s in range(1, n_frame)]
    odd = [hop(first, "vox", 1)] + [hop(x, "vox", 1) for x in firsts[1:]]
    ordered = [x for pair in zip(firsts, odd) for x in pair]
    code = call(
        functools.partial(second, blocks, n_frame),
        [shape((frames, LANE), BF)],
        (*ordered, *grams, corr, step),
        [pltpu.VMEM((modes, LANE), BF)],
        2 * frames * modes * LANE,
    )
    own_hops = [hop(code, "frame", s) for s in groups]
    half, rest = call(
        pack,
        [shape((blocks // 2, frames, LANE), BF), shape((blocks // 2 - 1, frames, LANE), BF)],
        (code, *[hop(code, "vox", m) for m in line]),
    )
    halves = [call(join, [half], (o, hop(rest, "frame", s))) for s, o in zip(groups, own_hops)]
    other = hop(half, "vox", 1)
    others = [hop(h, "vox", 1) for h in halves]
    codes, total, kept = call(
        own_group,
        [shape((frames, modes), BF), shape((own, width), F32), shape((own, width), BF)],
        (half, other, masked, batch, sup),
        flops=2 * frames * modes * width,
    )
    held = [pltpu.VMEM((frames, modes), BF)]
    work_size = 2 * frames * (modes + own) * width
    for i in range(n_frame - 1):
        args = (halves[i], others[i], batches[i], masked, total)
        if i < n_frame - 2:
            total = call(add_group, [shape((own, width), F32)], args, held, work_size)
        else:
            total = call(
                functools.partial(last_group, 1.0 / (frames * n_frame)),
                [shape((own, width), F32)],
                (*args, kept),
                [*held, pltpu.VMEM((own, width), F32), pltpu.SemaphoreType.DMA((4,))],
                work_size,
                to=pltpu.HBM,
            )
    return codes, total


def solution(mesh):
    placed = (P("frame", "vox"), P(None, "vox"), P(None, "vox"), P("frame"))
    return jax.shard_map(
        work,
        mesh=mesh,
        in_specs=placed,
        out_specs=(P("frame", None), P("frame", "vox")),
        check_vma=False,
    )
```
